32 devices in a mesh: dp: 8 (over z, y), expert: 4 (over x, core).
Axes of the slice: x: 2, y: 2, z: 4, core: 2. Of those that a mesh axis runs over, the one named last changes fastest.
Arguments:
- tokens: bfloat16 [8192, 1024], P(('dp', 'expert')), may hold values from -6 to 6
- out_cotangent: bfloat16 [8192, 1024], P(('dp', 'expert')), may hold values from -6 to 6
- segments: int32 [8192], P('dp'), may hold values from 0 to 15, never falling along the last dimension, each value on 1 to 1024 neighbouring positions
- routes: int32 [8192, 8], P(('dp', 'expert')), may hold values from 0 to 15, all different within a row; in each aligned block of 256 rows (0 to 255, 256 to 511, ...) at most 256 rows name the same one
- qkv_weight: float32 [1024, 2048], P(('dp', 'expert')), may hold values from -0.1875 to 0.1875
- qkv_mean: float32 [1024, 2048], P(('dp', 'expert')), may hold values from -6 to 6
- qkv_square: float32 [1024, 2048], P(('dp', 'expert')), may hold values from 1.5099494 to 15.099494
- proj_weight: float32 [1024, 1024], P(('dp', 'expert')), may hold values from -1.75 to 1.75
- proj_mean: float32 [1024, 1024], P(('dp', 'expert')), may hold values from -6 to 6
- proj_square: float32 [1024, 1024], P(('dp', 'expert')), may hold values from 0.802816 to 8.02816
- router_weight: float32 [1024, 16], P(('dp', 'expert')), may hold values from -0.1875 to 0.1875
- router_mean: float32 [1024, 16], P(('dp', 'expert')), may hold values from -56 to 56
- router_square: float32 [1024, 16], P(('dp', 'expert')), may hold values from 67.108864 to 671.0886
- norm_gains: float32 [2, 1024], P(None, ('dp', 'expert')), may hold values from 0.5 to 1.5
- gains_mean: float32 [2, 1024], P(None, ('dp', 'expert')), may hold values from -32 to 32
- gains_square: float32 [2, 1024], P(None, ('dp', 'expert')), may hold values from 26.2144 to 262.144
- gate_up_weight: float32 [1024, 16, 1024], P('dp', 'expert'), may hold values from -0.1875 to 0.1875
- gate_up_mean: float32 [1024, 16, 1024], P('dp', 'expert'), may hold values from -6 to 6
- gate_up_square: float32 [1024, 16, 1024], P('dp', 'expert'), may hold values from 0.2048 to 2.048
- down_weight: float32 [512, 16, 1024], P('dp', 'expert'), may hold values from -1.75 to 1.75
- down_mean: float32 [512, 16, 1024], P('dp', 'expert'), may hold values from -2 to 2
- down_square: float32 [512, 16, 1024], P('dp', 'expert'), may hold values from 0.01536 to 0.1536
Outputs:
- layer_out: bfloat16 [8192, 1024], P(('dp', 'expert'))
- token_grad: bfloat16 [8192, 1024], P(('dp', 'expert'))
- qkv_grad: float32 [1024, 2048], P(('dp', 'expert'))
- qkv_updated: float32 [1024, 2048], P(('dp', 'expert'))
- qkv_mean_out: float32 [1024, 2048], P(('dp', 'expert'))
- qkv_square_out: float32 [1024, 2048], P(('dp', 'expert'))
- proj_grad: float32 [1024, 1024], P(('dp', 'expert'))
- proj_updated: float32 [1024, 1024], P(('dp', 'expert'))
- proj_mean_out: float32 [1024, 1024], P(('dp', 'expert'))
- proj_square_out: float32 [1024, 1024], P(('dp', 'expert'))
- router_grad: float32 [1024, 16], P(('dp', 'expert'))
- router_updated: float32 [1024, 16], P(('dp', 'expert'))
- router_mean_out: float32 [1024, 16], P(('dp', 'expert'))
- router_square_out: float32 [1024, 16], P(('dp', 'expert'))
- gains_grad: float32 [2, 1024], P(None, ('dp', 'expert'))
- gains_updated: float32 [2, 1024], P(None, ('dp', 'expert'))
- gains_mean_out: float32 [2, 1024], P(None, ('dp', 'expert'))
- gains_square_out: float32 [2, 1024], P(None, ('dp', 'expert'))
- gate_up_grad: float32 [1024, 16, 1024], P('dp', 'expert')
- gate_up_updated: float32 [1024, 16, 1024], P('dp', 'expert')
- gate_up_mean_out: float32 [1024, 16, 1024], P('dp', 'expert')
- gate_up_square_out: float32 [1024, 16, 1024], P('dp', 'expert')
- down_grad: float32 [512, 16, 1024], P('dp', 'expert')
- down_updated: float32 [512, 16, 1024], P('dp', 'expert')
- down_mean_out: float32 [512, 16, 1024], P('dp', 'expert')
- down_square_out: float32 [512, 16, 1024], P('dp', 'expert')
The draws below stay inside these ranges and needn't reach their ends.
Inputs may be any that keep to these rules, and one draw needn't show every extreme that they name: `routes`: each row names 8 different experts. In the rows of one device (aligned blocks of 256 rows) an expert may be named by any number of rows up to all 256; some block has an expert named by all of its rows. `segments`: segment numbers never fall along the tokens; a segment may run on into the next sequence; one segment has exactly 1024 tokens.
All inputs are finite; a program needn't handle non-finite values.
Results may differ from the reference program's by a relative error of at most 0.015.
The reference program's roundings to bfloat16 on the way count: a program that leaves them out, or rounds other values in their place, can miss the bound.
Values may be sent and summed in bfloat16 or wider, within the bound.
No kernel may reach another device: no remote copies, remote signals or barrier semaphores. Data moves between devices by JAX's collectives and lax.ppermute only.
A program may use at most 192 MiB of HBM per device.

```python
import math
from functools import partial
import jax
import jax.numpy as jnp
import numpy as np
from jax import lax

D = 1024
HEADS = 16
KV_HEADS = 8
HEAD_DIM = 64
FF = 512
TOP = 8
TOK_DEV = 256
STEP = 10
EXPERTS = 16
SEQ = 1024
TOKENS = 8192
CAP = 256
N_DP = 8


def shard_levels(key, shape, split, least, largest):
    def one(axis_at, blocks):
        steps = jax.random.uniform(jax.random.fold_in(jax.random.fold_in(key, 6), axis_at), (blocks,), jnp.float32, least / len(split), largest / len(split))
        return jnp.repeat(jnp.exp(steps), shape[axis_at] // blocks).reshape((-1,) + (1,) * (len(shape) - axis_at - 1))

    factor_of = one(*split[0])
    for cut in split[1:]:
        factor_of = factor_of * one(*cut)
    return factor_of


def length_profile(amount, total, most, skew):
    weights = [(1 << 20) // math.isqrt(grade ** skew) + 1 for grade in range(2, amount + 1)]
    spare, holding = total - most - (amount - 1), [1] * (amount - 1)
    while spare > 0:
        movable = [i for i in range(amount - 1) if holding[i] < most]
        mass, remaining = sum([weights[i] for i in movable]), spare
        for i in movable:
            extra = min(most - holding[i], max(1, remaining * weights[i] // mass), spare)
            holding[i] = holding[i] + extra
            spare = spare - extra
    return np.array([most] + holding)


def ragged(stream_key, count, total, bound, skew):
    if count == 2:
        one = jax.random.randint(stream_key, (), max(1, total - bound), min(bound, total - 1) + 1)
        return jnp.stack([one, total - one])
    lengths = jnp.asarray(length_profile(count, total, bound, skew), jnp.int32)
    pairs = (count - 1) // 2
    giver, sink = lengths[1:1 + 2 * pairs:2], lengths[2:2 + 2 * pairs:2]
    slack = jnp.minimum(giver - 1, bound - sink)
    moved = jax.random.randint(jax.random.fold_in(stream_key, 1), (pairs,), 0, 1 << 20) % (slack + 1)
    lengths = lengths.at[1:1 + 2 * pairs:2].set(giver - moved).at[2:2 + 2 * pairs:2].set(sink + moved)
    return lengths[jax.random.permutation(jax.random.fold_in(stream_key, 2), count)]


def deal_out(key, own, number, rows, amount, top, limit, lean):
    ranking = jax.random.permutation(key, amount)
    crowded, usual = load_shares(amount, rows * top, limit, lean, True), load_shares(amount, rows * top, limit, lean, False)
    places = jnp.arange(amount)

    def named(tallies, turn):
        used = int((tallies > 0).sum())
        fixed = max(1, used // 4)
        shifted = fixed + (places - fixed + turn * (used - fixed)) % max(1, amount - fixed)
        return jnp.zeros((amount,), jnp.int32).at[ranking[jnp.where(places < fixed, places, shifted)]].set(jnp.asarray(tallies, jnp.int32))

    tallies = jnp.where(number % 4 == 0, named(crowded, number // 4), named(usual, number - number // 4 - 1))
    mixed = jax.random.permutation(jax.random.fold_in(own, 3), amount)
    donor, receiver = mixed[0:amount // 2 * 2:2], mixed[1:amount // 2 * 2:2]
    slack = jnp.minimum(tallies[donor] - 1, limit - tallies[receiver]) // 2
    slack = jnp.where((donor == ranking[0]) | (receiver == ranking[0]) | (tallies[receiver] == 0), 0, jnp.maximum(slack, 0))
    shifted = jax.random.randint(jax.random.fold_in(own, 4), (amount // 2,), 0, 1 << 20) % (slack + 1)
    tallies = tallies.at[donor].add(-shifted).at[receiver].add(shifted)
    members = jnp.searchsorted(jnp.cumsum(tallies), jnp.arange(rows * top), side="right").astype(jnp.int32)
    grid = members.reshape(top, rows).T
    grid = grid[jax.random.permutation(jax.random.fold_in(own, 1), rows)]
    turn = jax.random.randint(jax.random.fold_in(own, 2), (rows, 1), 0, top)
    return jnp.take_along_axis(grid, (jnp.arange(top)[None, :] + turn) % top, axis=1)


def load_shares(count, total, limit, skew, full):
    weights = [(1 << 20) // math.isqrt(rank ** skew) + 1 for rank in range(1, count + 1)]
    largest = limit if full else min(limit, max(-(-total // count), total * weights[0] // sum(weights)))
    least = 1 if total - largest >= count - 1 else 0
    holding, rest = [largest] + [least] * (count - 1), total - largest - least * (count - 1)
    while rest > 0:
        movable = [i for i in range(1, count) if holding[i] < largest] or [i for i in range(1, count) if holding[i] < limit]
        whole, budget = sum([weights[i] for i in movable]), rest
        for i in movable:
            extra = min(limit - holding[i], max(1, budget * weights[i] // whole), rest)
            holding[i] = holding[i] + extra
            rest = rest - extra
    return np.array(holding)


def normal_values(key, dims, width, most, split=(), dtype=jnp.bfloat16):
    gain = shard_levels(key, dims, split, -0.22, 0.18) if split else 1.0
    drawn = jax.random.normal(key, dims, jnp.float32) * width * gain
    return jnp.minimum(jnp.maximum(drawn, -most), most).astype(dtype)


def setup_inputs(seed: int = 0) -> dict:
    splits = jax.random.split(jax.random.key(seed), 23)
    tokens = normal_values(splits[0], (TOKENS, D), 1.0, 6.0, ((0, 32),))
    out_cotangent = normal_values(splits[1], (TOKENS, D), 1.0, 6.0, ((0, 32),))
    segments = jnp.searchsorted(jnp.cumsum(ragged(splits[2], 2 * N_DP, TOKENS, SEQ, 1)), jnp.arange(TOKENS), side="right").astype(jnp.int32)
    routes_keys = jax.random.split(jax.random.fold_in(splits[3], 1), TOKENS // TOK_DEV)
    routes_turns = jax.random.permutation(jax.random.fold_in(splits[3], 3), TOKENS // TOK_DEV)
    routes = jax.vmap(lambda own, number: deal_out(jax.random.fold_in(splits[3], 2), own, number, TOK_DEV, EXPERTS, TOP, CAP, 1))(routes_keys, routes_turns).reshape((TOKENS, TOP))
    qkv_weight = normal_values(splits[4], (D, (HEADS + 2 * KV_HEADS) * HEAD_DIM), D ** -0.5, 0.1875, ((0, 32),), jnp.float32)
    qkv_mean = normal_values(splits[5], (D, (HEADS + 2 * KV_HEADS) * HEAD_DIM), (0.00045 * (TOKENS * D) ** 0.5), 6.0, ((0, 32),), jnp.float32)
    qkv_square = jnp.clip(jnp.exp(math.log(15.099494) - 2.3025851 * jax.random.uniform(splits[6], (D, (HEADS + 2 * KV_HEADS) * HEAD_DIM), jnp.float32) ** shard_levels(splits[6], (D, (HEADS + 2 * KV_HEADS) * HEAD_DIM), ((0, 32),), -0.2, 0.2)), 1.5099494, 15.099494)
    proj_weight = normal_values(splits[7], (HEADS * HEAD_DIM, D), 0.12, 1.75, ((0, 32),), jnp.float32)
    proj_mean = normal_values(splits[8], (HEADS * HEAD_DIM, D), (0.0105 * TOKENS ** 0.5), 6.0, ((0, 32),), jnp.float32)
    proj_square = jnp.clip(jnp.exp(math.log(8.02816) - 2.3025851 * jax.random.uniform(splits[9], (HEADS * HEAD_DIM, D), jnp.float32) ** shard_levels(splits[9], (HEADS * HEAD_DIM, D), ((0, 32),), -0.2, 0.2)), 0.802816, 8.02816)
    router_weight = normal_values(splits[10], (D, EXPERTS), D ** -0.5, 0.1875, ((0, 32),), jnp.float32)
    router_mean = normal_values(splits[11], (D, EXPERTS), (0.003 * (TOKENS * D) ** 0.5), 56.0, ((0, 32),), jnp.float32)
    router_square = jnp.clip(jnp.exp(math.log(671.0886) - 2.3025851 * jax.random.uniform(splits[12], (D, EXPERTS), jnp.float32) ** shard_levels(splits[12], (D, EXPERTS), ((0, 32),), -0.2, 0.2)), 67.108864, 671.0886)
    norm_gains = jnp.clip(1.0 + 0.1 * jax.random.normal(splits[13], (2, D), jnp.float32), 0.5, 1.5)
    gains_mean = normal_values(splits[14], (2, D), (0.06 * TOKENS ** 0.5), 32.0, ((1, 32),), jnp.float32)
    gains_square = jnp.clip(jnp.exp(math.log(262.144) - 2.3025852 * jax.random.uniform(splits[15], (2, D), jnp.float32) ** shard_levels(splits[15], (2, D), ((1, 32),), -0.2, 0.2)), 26.2144, 262.144)
    gate_up_weight = normal_values(splits[16], (D, EXPERTS, 2 * FF), D ** -0.5, 0.1875, ((0, 8), (1, 4)), jnp.float32)
    gate_up_mean = normal_values(splits[17], (D, EXPERTS, 2 * FF), (0.0075 * (TOKENS * TOP / EXPERTS) ** 0.5), 6.0, ((0, 8), (1, 4)), jnp.float32)
    gate_up_square = jnp.clip(jnp.exp(math.log(2.048) - 2.3025852 * jax.random.uniform(splits[18], (D, EXPERTS, 2 * FF), jnp.float32) ** shard_levels(splits[18], (D, EXPERTS, 2 * FF), ((0, 8), (1, 4)), -0.2, 0.2)), 0.2048, 2.048)
    down_weight = normal_values(splits[19], (FF, EXPERTS, D), 0.12, 1.75, ((0, 8), (1, 4)), jnp.float32)
    down_mean = normal_values(splits[20], (FF, EXPERTS, D), (0.0165 * (TOKENS / (TOP * EXPERTS)) ** 0.5), 2.0, ((0, 8), (1, 4)), jnp.float32)
    down_square = jnp.clip(jnp.exp(math.log(0.1536) - 2.3025852 * jax.random.uniform(splits[21], (FF, EXPERTS, D), jnp.float32) ** shard_levels(splits[21], (FF, EXPERTS, D), ((0, 8), (1, 4)), -0.2, 0.2)), 0.01536, 0.1536)
    return dict(tokens=tokens, out_cotangent=out_cotangent, segments=segments, routes=routes, qkv_weight=qkv_weight, qkv_mean=qkv_mean, qkv_square=qkv_square, proj_weight=proj_weight, proj_mean=proj_mean, proj_square=proj_square, router_weight=router_weight, router_mean=router_mean, router_square=router_square, norm_gains=norm_gains, gains_mean=gains_mean, gains_square=gains_square, gate_up_weight=gate_up_weight, gate_up_mean=gate_up_mean, gate_up_square=gate_up_square, down_weight=down_weight, down_mean=down_mean, down_square=down_square)


norm_eps = 1e-06
res_scale = 0.22
rope_base = 10000.0
beta_one = 0.9
beta_two = 0.95
adam_eps = 1e-08
learn_rate = 0.04
gain_rate = 0.25
weight_decay = 0.1
highest = lax.Precision.HIGHEST

@jax.custom_vjp
def low(v):
    return lax.optimization_barrier(v.astype(jnp.bfloat16)).astype(jnp.float32)

@jax.custom_vjp
def low_back(v):
    return v

def low_keep(v):
    return (low(v), None)

def low_pass(kept, grad):
    return (grad,)

def back_keep(v):
    return (v, None)

def back_low(kept, grad):
    return (low(grad),)
low.defvjp(low_keep, low_pass)
low_back.defvjp(back_keep, back_low)

def rms_norm(values, gain_vec):
    inv_scale = lax.rsqrt(lax.optimization_barrier(jnp.mean(values * values, axis=-1, keepdims=True)) + norm_eps)
    return values * inv_scale * gain_vec

def rope_tables(positions, head_dim):
    half_dim = head_dim // 2
    frequency = rope_base ** (-(jnp.arange(half_dim).astype(jnp.float32) * 2.0 / head_dim))
    angles = positions.astype(jnp.float32)[:, None] * frequency[None, :]
    return (jnp.cos(angles), jnp.sin(angles))

def rotate(tensor, cosine_table, sine_table):
    half_dim = tensor.shape[-1] // 2
    front_half = tensor[..., :half_dim]
    back_half = tensor[..., half_dim:]
    cosine_row = cosine_table[:, None, :]
    sine_row = sine_table[:, None, :]
    return jnp.concatenate([front_half * cosine_row - back_half * sine_row, back_half * cosine_row + front_half * sine_row], axis=-1)

def attend(pieces):
    queries, keys_in, values_in, segment = pieces
    att_scale = HEAD_DIM ** (-0.5)
    scores = low_back(jnp.einsum('tkgd,skd->kgts', queries, keys_in, precision=highest) * att_scale)
    places = jnp.arange(segment.shape[0])
    allowed = ((segment[:, None] == segment[None, :]) & (places[None, :] <= places[:, None])).astype(jnp.float32)
    weights = jnp.exp(scores) * allowed
    weights = weights / lax.optimization_barrier(jnp.sum(weights, axis=-1, keepdims=True))
    return jnp.einsum('kgts,skd->tkgd', low(weights), values_in, precision=highest)

def forward(segments, routes, inputs, qkv_weight, proj_weight, router_weight, norm_gains, gate_up_weight, down_weight):
    qkv_low = low(qkv_weight)
    proj_low = low(proj_weight)
    router_low = low(router_weight)
    gains_low = low(norm_gains)
    gate_up_low = low(gate_up_weight)
    down_low = low(down_weight)
    q_width = HEADS * HEAD_DIM
    k_width = KV_HEADS * HEAD_DIM
    normed = low(rms_norm(inputs, gains_low[0]))
    qkv_out = low_back(jnp.dot(normed, qkv_low, precision=highest))
    cosine_table, sine_table = rope_tables(jnp.arange(SEQ), HEAD_DIM)
    queries = rotate(qkv_out[:, :q_width].reshape(N_DP, SEQ, HEADS, HEAD_DIM), cosine_table, sine_table)
    queries = low(queries).reshape(N_DP, SEQ, KV_HEADS, HEADS // KV_HEADS, HEAD_DIM)
    keys_in = low(rotate(qkv_out[:, q_width:q_width + k_width].reshape(N_DP, SEQ, KV_HEADS, HEAD_DIM), cosine_table, sine_table))
    values_in = low(qkv_out[:, q_width + k_width:].reshape(N_DP, SEQ, KV_HEADS, HEAD_DIM))
    attended = lax.map(jax.checkpoint(attend), (queries, keys_in, values_in, segments.reshape(N_DP, SEQ)))
    attended = low(low_back(attended.reshape(TOKENS, q_width)))
    branch = low_back(jnp.dot(attended, proj_low, precision=highest))
    hidden = inputs + res_scale * branch
    normed_two = low(rms_norm(hidden, gains_low[1]))
    logits = low_back(jnp.dot(normed_two, router_low, precision=highest))
    chosen = lax.optimization_barrier(jnp.sum((routes[:, :, None] == jnp.arange(EXPERTS)[None, None, :]).astype(jnp.float32), axis=1))
    raw_gate = jnp.exp(logits) * chosen
    router_probs = raw_gate / lax.optimization_barrier(jnp.sum(raw_gate, axis=-1, keepdims=True))

    def expert_step(running, parts):
        gate_up, down_part, share = parts
        entry_rows = low_back(normed_two)
        gate_up_out = low_back(jnp.dot(entry_rows, gate_up, precision=highest))
        unit_values = low(jax.nn.silu(gate_up_out[:, :FF]) * gate_up_out[:, FF:])
        result = low(low_back(jnp.dot(unit_values, down_part, precision=highest)))
        return (running + share[:, None] * result, None)
    mixture, unused = lax.scan(jax.checkpoint(expert_step), jnp.zeros_like(hidden), (jnp.moveaxis(gate_up_low, 1, 0), jnp.moveaxis(down_low, 1, 0), router_probs.T))
    return hidden + res_scale * mixture

def adamw(weight, gradient, mean_in, square, step_rate, decay_rate):
    mean_new = beta_one * mean_in + (1.0 - beta_one) * gradient
    square_new = beta_two * square + (1.0 - beta_two) * gradient * gradient
    fix_one = 1.0 - beta_one ** STEP
    fix_two = 1.0 - beta_two ** STEP
    update = mean_new / fix_one / (jnp.sqrt(square_new / fix_two) + adam_eps)
    return (weight - step_rate * (update + decay_rate * weight), mean_new, square_new)

def reference(tokens, out_cotangent, segments, routes, qkv_weight, qkv_mean, qkv_square, proj_weight, proj_mean, proj_square, router_weight, router_mean, router_square, norm_gains, gains_mean, gains_square, gate_up_weight, gate_up_mean, gate_up_square, down_weight, down_mean, down_square):
    primal, pullback = jax.vjp(partial(forward, segments, routes), tokens.astype(jnp.float32), qkv_weight, proj_weight, router_weight, norm_gains, gate_up_weight, down_weight)
    gradients = pullback(out_cotangent.astype(jnp.float32))
    qkv_new = adamw(qkv_weight, gradients[1], qkv_mean, qkv_square, learn_rate, weight_decay)
    proj_new = adamw(proj_weight, gradients[2], proj_mean, proj_square, learn_rate, weight_decay)
    router_new = adamw(router_weight, gradients[3], router_mean, router_square, learn_rate, weight_decay)
    gains_new = adamw(norm_gains, gradients[4], gains_mean, gains_square, gain_rate, 0.0)
    gate_up_new = adamw(gate_up_weight, gradients[5], gate_up_mean, gate_up_square, learn_rate, weight_decay)
    down_new = adamw(down_weight, gradients[6], down_mean, down_square, learn_rate, weight_decay)
    return (primal.astype(jnp.bfloat16), gradients[0].astype(jnp.bfloat16), gradients[1], qkv_new[0], qkv_new[1], qkv_new[2], gradients[2], proj_new[0], proj_new[1], proj_new[2], gradients[3], router_new[0], router_new[1], router_new[2], gradients[4], gains_new[0], gains_new[1], gains_new[2], gradients[5], gate_up_new[0], gate_up_new[1], gate_up_new[2], gradients[6], down_new[0], down_new[1], down_new[2])
```

```python
import functools

import jax
import jax.numpy as jnp
from jax import lax
from jax.experimental import pallas as pl
from jax.experimental.pallas import tpu as pltpu
from jax.sharding import PartitionSpec as P

HEADS = 16
KV_HEADS = 8
HEAD_DIM = 64
STEP = 10

norm_eps = 1e-06
res_scale = 0.22
rope_base = 10000.0
beta_one = 0.9
beta_two = 0.95
adam_eps = 1e-08
learn_rate = 0.04
gain_rate = 0.25
weight_decay = 0.1

bf16 = jnp.bfloat16
f32 = jnp.float32
BLK = 256
PACK = 128


def adamw(weight, gradient, mean_in, square, step_rate, decay_rate):
    mean_new = beta_one * mean_in + (1.0 - beta_one) * gradient
    square_new = beta_two * square + (1.0 - beta_two) * gradient * gradient
    fix_one = 1.0 - beta_one**STEP
    fix_two = 1.0 - beta_two**STEP
    update = mean_new / fix_one / (jnp.sqrt(square_new / fix_two) + adam_eps)
    return (weight - step_rate * (update + decay_rate * weight), mean_new, square_new)


def xor_send(value, mask):
    size = lax.axis_size("expert")
    return lax.ppermute(value, "expert", [(e, e ^ mask) for e in range(size)])


def group_gather(value):
    near = xor_send(value, 1)
    far = xor_send(value, 2)
    both = xor_send(far, 1)
    return [value, near, far, both]


def in_order(blocks, member, axis):
    width = blocks[0].shape[axis]
    shape = list(blocks[0].shape)
    shape[axis] = width * len(blocks)
    out = jnp.zeros(tuple(shape), blocks[0].dtype)
    for r, block in enumerate(blocks):
        out = lax.dynamic_update_slice_in_dim(out, block, (member ^ r) * width, axis)
    return out


def group_reduce(pick):
    near = xor_send(jnp.stack([pick(1), pick(3)]).astype(bf16), 1)
    far_sum = (pick(2) + near[1].astype(f32)).astype(bf16)
    far = xor_send(far_sum, 2)
    return pick(0) + near[0].astype(f32) + far.astype(f32)


def ring_order(size):
    if size == 8:
        return [0, 2, 4, 6, 7, 5, 3, 1]
    return list(range(size))


class Ring:
    def __init__(self):
        self.size = lax.axis_size("dp")
        self.order = ring_order(self.size)
        place = [0] * self.size
        for i, d in enumerate(self.order):
            place[d] = i
        self.place = jnp.asarray(place, jnp.int32)[lax.axis_index("dp")]
        self.order_table = jnp.asarray(self.order, jnp.int32)
        n = self.size
        self.up = [(self.order[i], self.order[(i + 1) % n]) for i in range(n)]
        self.down = [(self.order[(i + 1) % n], self.order[i]) for i in range(n)]

    def device(self, offset):
        return self.order_table[(self.place + offset) % self.size]

    def send_up(self, value):
        return lax.ppermute(value, "dp", self.up)

    def send_down(self, value):
        return lax.ppermute(value, "dp", self.down)

    def gather(self, value):
        half = self.size // 2
        pieces = {0: value}
        left = right = value
        for k in range(1, half):
            left, right = self.send_up(left), self.send_down(right)
            pieces[-k], pieces[k] = left, right
        low = self.send_up(left[:1])
        high = self.send_down(right[1:])
        return pieces, low, high

    def reduce(self, pick):
        half = self.size // 2
        up = self.send_up(pick(half, 0, 1))
        down = self.send_down(pick(half, 1, 2))
        for k in range(half - 1, 0, -1):
            mine_up, mine_down = pick(k, 0, 2), pick(-k, 0, 2)
            if k == half - 1:
                sum_up = jnp.concatenate(
                    [(mine_up[:1].astype(f32) + up.astype(f32)).astype(bf16), mine_up[1:]]
                )
                sum_down = jnp.concatenate(
                    [mine_down[:1], (mine_down[1:].astype(f32) + down.astype(f32)).astype(bf16)]
                )
            else:
                sum_up = (mine_up.astype(f32) + up.astype(f32)).astype(bf16)
                sum_down = (mine_down.astype(f32) + down.astype(f32)).astype(bf16)
            up, down = self.send_up(sum_up), self.send_down(sum_down)
        return pick(0, 0, 2).astype(f32) + up.astype(f32) + down.astype(f32)


def cost(flops, bytes_accessed, transcendentals=0):
    return pl.CostEstimate(
        flops=int(flops), bytes_accessed=int(bytes_accessed), transcendentals=int(transcendentals)
    )


def mm(a, b):
    return lax.dot_general(a, b, (((1,), (0,)), ((), ())), preferred_element_type=f32)


def mm_nt(a, b):
    return lax.dot_general(a, b, (((1,), (1,)), ((), ())), preferred_element_type=f32)


def mm_tn(a, b):
    return lax.dot_general(a, b, (((0,), (0,)), ((), ())), preferred_element_type=f32)


def swap_halves(x):
    lane = lax.broadcasted_iota(jnp.int32, x.shape, 1)
    width = x.shape[1]
    half = HEAD_DIM // 2
    ahead = pltpu.roll(x, width - half, 1)
    behind = pltpu.roll(x, half, 1)
    return jnp.where(lane % HEAD_DIM < half, ahead, behind)


def qkv_kernel(x_ref, w_ref, gain_ref, cos_ref, sin_ref, normed_ref, inv_ref, q_ref, k_ref, v_ref):
    x = x_ref[...].astype(f32)
    inv = lax.rsqrt(jnp.mean(x * x, axis=-1, keepdims=True) + norm_eps)
    normed = (x * inv * gain_ref[0:1, :]).astype(bf16)
    normed_ref[...] = normed
    inv_ref[...] = inv
    out = mm(normed, w_ref[...])
    cosine, sine = cos_ref[...], sin_ref[...]
    q_heads, kv_heads = q_ref.shape[0], k_ref.shape[0]
    scale = HEAD_DIM ** (-0.5)
    for t in range((q_heads + 2 * kv_heads) // 2):
        part = out[:, t * 128 : (t + 1) * 128]
        first = 2 * t
        if first < q_heads + kv_heads:
            part = part * cosine + swap_halves(part) * sine
        if first < q_heads:
            part = (part.astype(bf16).astype(f32) * scale).astype(bf16)
            q_ref[first] = part[:, :HEAD_DIM]
            q_ref[first + 1] = part[:, HEAD_DIM:]
        else:
            part = part.astype(bf16)
            ref, first = (k_ref, first - q_heads)
            if first >= kv_heads:
                ref, first = v_ref, first - kv_heads
            ref[first] = part[:, :HEAD_DIM]
            ref[first + 1] = part[:, HEAD_DIM:]


def qkv_call(x, weights, gains, cosine, sine, q_heads, kv_heads):
    seq, dim = x.shape
    width = (q_heads + 2 * kv_heads) * HEAD_DIM
    rows = lambda i: (i, 0)
    whole = lambda i: (0, 0)
    head = lambda i: (0, i, 0)
    return pl.pallas_call(
        qkv_kernel,
        grid=(seq // BLK,),
        in_specs=[
            pl.BlockSpec((BLK, dim), rows),
            pl.BlockSpec((dim, width), whole),
            pl.BlockSpec((2, dim), whole),
            pl.BlockSpec((BLK, 128), rows),
            pl.BlockSpec((BLK, 128), rows),
        ],
        out_specs=[
            pl.BlockSpec((BLK, dim), rows),
            pl.BlockSpec((BLK, 1), rows),
            pl.BlockSpec((q_heads, BLK, HEAD_DIM), head),
            pl.BlockSpec((kv_heads, BLK, HEAD_DIM), head),
            pl.BlockSpec((kv_heads, BLK, HEAD_DIM), head),
        ],
        out_shape=[
            jax.ShapeDtypeStruct((seq, dim), bf16),
            jax.ShapeDtypeStruct((seq, 1), f32),
            jax.ShapeDtypeStruct((q_heads, seq, HEAD_DIM), bf16),
            jax.ShapeDtypeStruct((kv_heads, seq, HEAD_DIM), bf16),
            jax.ShapeDtypeStruct((kv_heads, seq, HEAD_DIM), bf16),
        ],
        cost_estimate=cost(2 * seq * dim * width, 6 * seq * dim),
        name="qkv",
    )(x, weights, gains, cosine, sine)


def mask_of(i, j, seg_col, seg_row):
    row = lax.broadcasted_iota(jnp.int32, (BLK, BLK), 0) + i * BLK
    col = lax.broadcasted_iota(jnp.int32, (BLK, BLK), 1) + j * BLK
    return (col <= row) & (seg_col == seg_row)


def attention_kernel(first_ref, q_ref, k_ref, v_ref, segc_ref, segr_ref, att_ref, inv_ref, acc, tot):
    i = pl.program_id(0)
    heads = q_ref.shape[0]
    share = heads // k_ref.shape[0]
    acc[...] = jnp.zeros_like(acc)
    tot[...] = jnp.zeros_like(tot)
    seg_col = segc_ref[...]

    def step(j, carry):
        at = pl.ds(pl.multiple_of(j * BLK, BLK), BLK)
        keep = mask_of(i, j, seg_col, segr_ref[:, at])
        for h in range(heads):
            raw = jnp.exp(mm_nt(q_ref[h], k_ref[h // share, at, :]))
            raw = jnp.where(keep, raw, 0.0)
            tot[h] += jnp.sum(raw, axis=-1, keepdims=True)
            acc[h] += mm(raw.astype(bf16), v_ref[h // share, at, :])
        return carry

    lax.fori_loop(first_ref[i], i + 1, step, 0)
    for h in range(heads):
        inv = 1.0 / tot[h]
        att_ref[:, h * HEAD_DIM : (h + 1) * HEAD_DIM] = (acc[h] * inv).astype(bf16)
        inv_ref[h] = inv


def attention_call(first, q, k, v, seg_col, seg_row):
    heads, seq, _ = q.shape
    kv = k.shape[0]
    return pl.pallas_call(
        attention_kernel,
        grid_spec=pltpu.PrefetchScalarGridSpec(
            num_scalar_prefetch=1,
            grid=(seq // BLK,),
            in_specs=[
                pl.BlockSpec((heads, BLK, HEAD_DIM), lambda i, f: (0, i, 0)),
                pl.BlockSpec((kv, seq, HEAD_DIM), lambda i, f: (0, 0, 0)),
                pl.BlockSpec((kv, seq, HEAD_DIM), lambda i, f: (0, 0, 0)),
                pl.BlockSpec((BLK, 1), lambda i, f: (i, 0)),
                pl.BlockSpec((1, seq), lambda i, f: (0, 0)),
            ],
            out_specs=[
                pl.BlockSpec((BLK, heads * HEAD_DIM), lambda i, f: (i, 0)),
                pl.BlockSpec((heads, BLK, 1), lambda i, f: (0, i, 0)),
            ],
            scratch_shapes=[
                pltpu.VMEM((heads, BLK, HEAD_DIM), f32),
                pltpu.VMEM((heads, BLK, 1), f32),
            ],
        ),
        out_shape=[
            jax.ShapeDtypeStruct((seq, heads * HEAD_DIM), bf16),
            jax.ShapeDtypeStruct((heads, seq, 1), f32),
        ],
        cost_estimate=cost(2 * heads * seq * seq * 256, 4 * seq * 512, heads * seq * seq // 2),
        name="attention",
    )(first, q, k, v, seg_col, seg_row)


def attention_back_kernel(
    first_ref, q_ref, k_ref, v_ref, att_ref, inv_ref, gbr_ref, proj_ref, segc_ref, segr_ref,
    cos_ref, sin_ref, cosa_ref, sina_ref, gq_ref, gk_ref, gv_ref, ga, delta, gq_acc, gk_acc, gv_acc,
):
    i = pl.program_id(0)
    heads, kv = q_ref.shape[0], k_ref.shape[0]
    share = heads // kv

    @pl.when(i == 0)
    def _():
        gk_acc[...] = jnp.zeros_like(gk_acc)
        gv_acc[...] = jnp.zeros_like(gv_acc)

    grad_att = mm_nt(gbr_ref[...], proj_ref[...]).astype(bf16)
    for h in range(heads):
        lanes = slice(h * HEAD_DIM, (h + 1) * HEAD_DIM)
        one = grad_att[:, lanes]
        ga[h] = one
        delta[h] = jnp.sum(one.astype(f32) * att_ref[:, lanes].astype(f32), axis=-1, keepdims=True)
    gq_acc[...] = jnp.zeros_like(gq_acc)
    seg_col = segc_ref[...]

    def step(j, carry):
        at = pl.ds(pl.multiple_of(j * BLK, BLK), BLK)
        keep = mask_of(i, j, seg_col, segr_ref[:, at])
        for h in range(heads):
            g = h // share
            key, value = k_ref[g, at, :], v_ref[g, at, :]
            prob = jnp.exp(mm_nt(q_ref[h], key)) * inv_ref[h]
            prob = jnp.where(keep, prob, 0.0)
            gw = mm_nt(ga[h], value)
            gs = (prob * (gw - delta[h])).astype(bf16)
            gq_acc[h] += mm(gs, key)
            gk_acc[g, at, :] += mm_tn(gs, q_ref[h])
            gv_acc[g, at, :] += mm_tn(prob.astype(bf16), ga[h])
        return carry

    lax.fori_loop(first_ref[i], i + 1, step, 0)
    scale = HEAD_DIM ** (-0.5)

    def back(pair, cosine, sine):
        return (pair * cosine - swap_halves(pair) * sine).astype(bf16)

    for t in range(heads // 2):
        pair = jnp.concatenate([gq_acc[2 * t], gq_acc[2 * t + 1]], axis=-1) * scale
        gq_ref[:, t * 128 : (t + 1) * 128] = back(pair, cos_ref[...], sin_ref[...])

    @pl.when(i == pl.num_programs(0) - 1)
    def _():
        for t in range(kv // 2):
            lanes = slice(t * 128, (t + 1) * 128)
            pair = jnp.concatenate([gk_acc[2 * t], gk_acc[2 * t + 1]], axis=-1)
            gk_ref[:, lanes] = back(pair, cosa_ref[...], sina_ref[...])
            pair = jnp.concatenate([gv_acc[2 * t], gv_acc[2 * t + 1]], axis=-1)
            gv_ref[:, lanes] = pair.astype(bf16)


def attention_back_call(first, q, k, v, att, inv, gbr, proj, seg_col, seg_row, cosine, sine):
    heads, seq, _ = q.shape
    kv = k.shape[0]
    dim = gbr.shape[1]
    row = lambda i, f: (i, 0)
    whole = lambda i, f: (0, 0)
    head = lambda i, f: (0, i, 0)
    heads_all = lambda i, f: (0, 0, 0)
    return pl.pallas_call(
        attention_back_kernel,
        grid_spec=pltpu.PrefetchScalarGridSpec(
            num_scalar_prefetch=1,
            grid=(seq // BLK,),
            in_specs=[
                pl.BlockSpec((heads, BLK, HEAD_DIM), head),
                pl.BlockSpec((kv, seq, HEAD_DIM), heads_all),
                pl.BlockSpec((kv, seq, HEAD_DIM), heads_all),
                pl.BlockSpec((BLK, heads * HEAD_DIM), row),
                pl.BlockSpec((heads, BLK, 1), head),
                pl.BlockSpec((BLK, dim), row),
                pl.BlockSpec((heads * HEAD_DIM, dim), whole),
                pl.BlockSpec((BLK, 1), row),
                pl.BlockSpec((1, seq), whole),
                pl.BlockSpec((BLK, 128), row),
                pl.BlockSpec((BLK, 128), row),
                pl.BlockSpec((seq, 128), whole),
                pl.BlockSpec((seq, 128), whole),
            ],
            out_specs=[
                pl.BlockSpec((BLK, heads * HEAD_DIM), row),
                pl.BlockSpec((seq, kv * HEAD_DIM), whole),
                pl.BlockSpec((seq, kv * HEAD_DIM), whole),
            ],
            scratch_shapes=[
                pltpu.VMEM((heads, BLK, HEAD_DIM), bf16),
                pltpu.VMEM((heads, BLK, 1), f32),
                pltpu.VMEM((heads, BLK, HEAD_DIM), f32),
                pltpu.VMEM((kv, seq, HEAD_DIM), f32),
                pltpu.VMEM((kv, seq, HEAD_DIM), f32),
            ],
        ),
        out_shape=[
            jax.ShapeDtypeStruct((seq, heads * HEAD_DIM), bf16),
            jax.ShapeDtypeStruct((seq, kv * HEAD_DIM), bf16),
            jax.ShapeDtypeStruct((seq, kv * HEAD_DIM), bf16),
        ],
        cost_estimate=cost(2 * heads * seq * seq * 640, 4 * seq * 1024, heads * seq * seq // 2),
        name="attention_back",
    )(first, q, k, v, att, inv, gbr, proj, seg_col, seg_row, cosine, sine, cosine, sine)


def expert_kernel(
    n_pieces, whole_pieces, info_ref, *refs,
):
    pieces = refs[:n_pieces]
    x_ref, xa_ref, g_ref, ga_ref, probs_ref, mix_in, ge_in, gsh_in = refs[n_pieces : n_pieces + 8]
    mix_ref, ge_ref, gsh_ref, grads_ref = refs[n_pieces + 8 : n_pieces + 12]
    w, down, gboth, scaled = refs[n_pieces + 12 :]
    i = pl.program_id(0)
    dim = w.shape[0]
    ff = down.shape[0]
    n = grads_ref.shape[1]
    wr, dr = dim // n, ff // n

    @pl.when(i == 0)
    def _():
        for t, piece in enumerate(pieces):
            at = info_ref[t + 1]
            w[pl.ds(pl.multiple_of(at * wr, wr), wr), :] = piece[0, :wr, :]
            down[pl.ds(pl.multiple_of(at * dr, dr), dr), :] = piece[0, wr:, :]

    x, g = x_ref[...], g_ref[...]
    lane = lax.broadcasted_iota(jnp.int32, probs_ref.shape, 1)
    mine = lane == info_ref[0]
    share = jnp.sum(jnp.where(mine, probs_ref[...], 0.0), axis=-1, keepdims=True)
    both = mm(x, w[...])
    gate, up = both[:, :ff], both[:, ff:]
    raw = mm_nt(g, down[...]) * res_scale
    sg = 1.0 / (1.0 + jnp.exp(-gate))
    act = gate * sg
    units = act * up
    gsh_ref[...] = gsh_in[...] + jnp.where(mine, jnp.sum(units * raw, axis=-1, keepdims=True), 0.0)
    here = pl.ds(pl.multiple_of(i * BLK, BLK), BLK)
    us = (units * share).astype(bf16)
    scaled[here, :] = us
    gunits = raw * share
    gg = (gunits * up * sg * (1.0 + gate * (1.0 - sg))).astype(bf16)
    gu = (gunits * act).astype(bf16)
    gboth[here, :ff] = gg
    gboth[here, ff:] = gu
    mix_ref[...] = mix_in[...] + mm(us, down[...])
    ge_ref[...] = ge_in[...] + mm_nt(gboth[here, :], w[...])

    @pl.when(i == pl.num_programs(0) - 1)
    def _():
        gw = mm_tn(xa_ref[...], gboth[...]).astype(bf16)
        for d in range(n):
            grads_ref[0, d, :wr, :] = gw[d * wr : (d + 1) * wr]
        gd = (mm_tn(scaled[...], ga_ref[...]) * res_scale).astype(bf16)
        for d in range(n):
            grads_ref[0, d, wr:, :] = gd[d * dr : (d + 1) * dr]


def expert_call(info, pieces, x, g, probs, mix, ge, gsh, n):
    seq, dim = x.shape
    rows = pieces[0][0].shape[1]
    ff = rows * n - dim
    row = lambda i, f: (i, 0)
    whole = lambda i, f: (0, 0)
    piece_specs = [
        pl.BlockSpec((1, rows, dim), lambda i, f, at=at: (at, 0, 0)) for _, at in pieces
    ]
    count = len(pieces)
    return pl.pallas_call(
        functools.partial(expert_kernel, count, None),
        grid_spec=pltpu.PrefetchScalarGridSpec(
            num_scalar_prefetch=1,
            grid=(seq // BLK,),
            in_specs=piece_specs
            + [
                pl.BlockSpec((BLK, dim), row),
                pl.BlockSpec((seq, dim), whole),
                pl.BlockSpec((BLK, dim), row),
                pl.BlockSpec((seq, dim), whole),
                pl.BlockSpec((BLK, PACK), row),
                pl.BlockSpec((BLK, dim), row),
                pl.BlockSpec((BLK, dim), row),
                pl.BlockSpec((BLK, PACK), row),
            ],
            out_specs=[
                pl.BlockSpec((BLK, dim), row),
                pl.BlockSpec((BLK, dim), row),
                pl.BlockSpec((BLK, PACK), row),
                pl.BlockSpec((1, n, rows, dim), lambda i, f: (0, 0, 0, 0)),
            ],
            scratch_shapes=[
                pltpu.VMEM((dim, 2 * ff), bf16),
                pltpu.VMEM((ff, dim), bf16),
                pltpu.VMEM((seq, 2 * ff), bf16),
                pltpu.VMEM((seq, ff), bf16),
            ],
        ),
        out_shape=[
            jax.ShapeDtypeStruct((seq, dim), f32),
            jax.ShapeDtypeStruct((seq, dim), f32),
            jax.ShapeDtypeStruct((seq, PACK), f32),
            jax.ShapeDtypeStruct((1, n, rows, dim), bf16),
        ],
        cost_estimate=cost(2 * seq * dim * ff * 9, 40 * seq * dim, seq * ff),
        compiler_params=pltpu.CompilerParams(vmem_limit_bytes=60 << 20),
        name="expert",
    )(info, *[a for a, _ in pieces], x, x, g, g, probs, mix, ge, gsh)


def on_device(
    tokens,
    out_cotangent,
    segments,
    routes,
    qkv_weight,
    qkv_mean,
    qkv_square,
    proj_weight,
    proj_mean,
    proj_square,
    router_weight,
    router_mean,
    router_square,
    norm_gains,
    gains_mean,
    gains_square,
    gate_up_weight,
    gate_up_mean,
    gate_up_square,
    down_weight,
    down_mean,
    down_square,
):
    groups = lax.axis_size("expert")
    n = lax.axis_size("dp")
    member = lax.axis_index("expert")
    ring = Ring()
    tok_rows, dim = tokens.shape
    seq = segments.shape[0]
    experts_all = router_weight.shape[1]
    experts_here = gate_up_weight.shape[1]
    lines = qkv_weight.shape[0]
    q_heads, kv_heads = HEADS // groups, KV_HEADS // groups
    qw, kw = q_heads * HEAD_DIM, kv_heads * HEAD_DIM
    cols = qw + 2 * kw
    wide = cols + PACK

    pack = jnp.concatenate(
        [router_weight, norm_gains.T, jnp.zeros((lines, PACK - experts_all - 2), f32)], axis=1
    ).astype(bf16)
    low = qkv_weight.astype(bf16)
    full_q, full_k = HEADS * HEAD_DIM, KV_HEADS * HEAD_DIM
    by_member = jnp.stack(
        [
            jnp.concatenate(
                [
                    low[:, j * qw : (j + 1) * qw],
                    low[:, full_q + j * kw : full_q + (j + 1) * kw],
                    low[:, full_q + full_k + j * kw : full_q + full_k + (j + 1) * kw],
                    pack,
                ],
                axis=1,
            )
            for j in range(groups)
        ]
    )
    take = lambda r: lax.dynamic_index_in_dim(by_member, member ^ r, 0, keepdims=False)
    blocks = [take(0)] + [xor_send(take(r), r) for r in range(1, groups)]
    dense = jnp.concatenate([in_order(blocks, member, 1), proj_weight.astype(bf16)], axis=1)
    token_blocks = group_gather(tokens)
    halves = dense.reshape(2, lines // 2, groups * wide + dim)
    pieces, low_half, high_half = ring.gather(halves)
    dense_all = jnp.zeros((n, 2, lines // 2, groups * wide + dim), bf16)
    for k, piece in pieces.items():
        dense_all = lax.dynamic_update_slice(dense_all, piece[None], (ring.device(k), 0, 0, 0))
    far = ring.device(n // 2)
    dense_all = lax.dynamic_update_slice(dense_all, low_half[None], (far, 0, 0, 0))
    dense_all = lax.dynamic_update_slice(dense_all, high_half[None], (far, 1, 0, 0))
    dense_all = dense_all.reshape(n, lines, groups * wide + dim)
    qkv_full = jnp.stack(
        [dense_all[:, :, e * wide : (e + 1) * wide] for e in range(groups)], axis=1
    ).reshape(dim, wide)
    proj_rows = dense_all[:, :, groups * wide :]
    router_full = qkv_full[:, cols : cols + PACK]
    gains_full = qkv_full[:, cols + experts_all : cols + experts_all + 2].T.astype(f32)
    gain_one, gain_two = gains_full[0], gains_full[1]

    low_gate_up = jnp.moveaxis(gate_up_weight.astype(bf16), 1, 0)
    low_down = jnp.moveaxis(down_weight.astype(bf16), 1, 0)
    shard = jnp.concatenate([low_gate_up, low_down], axis=1)
    streams = [ring.gather(shard[s : s + 2]) for s in range(0, experts_here, 2)]

    x_all = in_order(token_blocks, member, 0)
    half_dim = HEAD_DIM // 2
    frequency = rope_base ** (-(jnp.arange(half_dim).astype(f32) * 2.0 / HEAD_DIM))
    angles = jnp.arange(seq, dtype=jnp.int32).astype(f32)[:, None] * frequency[None, :]
    cosine, sine = jnp.cos(angles), jnp.sin(angles)
    cosine = jnp.tile(cosine, (1, 4))
    sine = jnp.tile(jnp.concatenate([-sine, sine], axis=1), (1, 2))
    seg_col, seg_row = segments[:, None], segments[None, :]
    starts = segments.reshape(seq // BLK, BLK)[:, 0]
    first = jnp.sum((segments[None, :] < starts[:, None]).astype(jnp.int32), axis=1) // BLK
    normed, inv_one, q, k, v = qkv_call(x_all, qkv_full, gains_full, cosine, sine, q_heads, kv_heads)
    att, inv_tot = attention_call(first, q, k, v, seg_col, seg_row)

    proj_blocks = group_gather(proj_rows)
    proj_full = in_order([b[:, None] for b in proj_blocks], member, 1).reshape(dim, dim)
    att_all = in_order(group_gather(att), member, 1)
    branch = jnp.dot(att_all, proj_full, preferred_element_type=f32)
    hidden_all = x_all.astype(f32) + res_scale * branch
    inv_two_all = lax.rsqrt(jnp.mean(hidden_all * hidden_all, axis=-1, keepdims=True) + norm_eps)
    normed_two = (hidden_all * inv_two_all * gain_two).astype(bf16)

    expert_ids = jnp.arange(PACK, dtype=jnp.int32)
    chosen = jnp.sum((routes[:, :, None] == expert_ids[None, None, :]).astype(f32), axis=1)
    extra_blocks = group_gather(jnp.concatenate([out_cotangent, chosen.astype(bf16)], axis=1))
    extra = in_order(extra_blocks, member, 0)
    gout_all, chosen_all = extra[:, :dim], extra[:, dim:].astype(f32)
    logits = jnp.dot(normed_two, router_full, preferred_element_type=f32)
    raw_gate = jnp.where(chosen_all > 0.0, jnp.exp(logits), 0.0)
    probs_all = raw_gate / jnp.sum(raw_gate, axis=-1, keepdims=True)

    mix = jnp.zeros((seq, dim), f32)
    ge = jnp.zeros((seq, dim), f32)
    gsh = jnp.zeros((seq, PACK), f32)
    local_grads = []
    for s, (weights, low_part, high_part) in enumerate(streams):
        for h in range(2):
            e = 2 * s + h
            devices = [member * experts_here + e] + [ring.device(k) for k in weights] + [far]
            parts = [(w, h) for w in weights.values()] + [(low_part if h == 0 else high_part, 0)]
            info = jnp.stack(devices).astype(jnp.int32)
            mix, ge, gsh, grads = expert_call(
                info, parts, normed_two, gout_all, probs_all, mix, ge, gsh, n
            )
            local_grads.append(grads)

    offset = member * tok_rows
    mine = lambda a, r: lax.dynamic_slice_in_dim(a, (member ^ r) * tok_rows, tok_rows, 0)
    own = lambda a: mine(a, 0)
    high = gsh.astype(bf16).astype(f32)
    ge_wide = jnp.concatenate([ge, high, gsh - high], axis=1)
    back = group_reduce(lambda r: mine(ge_wide, r))
    entry, grad_probs = back[:, :dim], back[:, dim : dim + PACK] + back[:, dim + PACK :]
    router_probs = own(probs_all)
    hidden, inv_two = own(hidden_all), own(inv_two_all)
    grad_logits = router_probs * (
        grad_probs - jnp.sum(router_probs * grad_probs, axis=-1, keepdims=True)
    )
    grad_logits = grad_logits.astype(bf16)
    router_term = jnp.einsum("td,te->de", own(normed_two), grad_logits, preferred_element_type=f32)
    grad_normed_two = entry + jnp.einsum(
        "te,de->td", grad_logits, router_full, preferred_element_type=f32
    )
    grad_out = out_cotangent.astype(f32)
    scaled_two = grad_normed_two * gain_two
    gain_two_term = jnp.sum(grad_normed_two * hidden * inv_two, axis=0)
    grad_hidden = (
        grad_out
        + inv_two * scaled_two
        - hidden
        * (inv_two * inv_two * inv_two)
        * jnp.mean(scaled_two * hidden, axis=-1, keepdims=True)
    )
    grad_branch = (res_scale * grad_hidden).astype(bf16)
    grad_branch_all = in_order(group_gather(grad_branch), member, 0)

    mixture = group_reduce(lambda r: mine(mix, r))
    layer_out = (hidden + res_scale * mixture).astype(bf16)

    proj_own = lax.dynamic_slice_in_dim(proj_full, member * qw, qw, 0)
    proj_term = jnp.einsum("tq,td->qd", att, grad_branch_all, preferred_element_type=f32)
    gq, gk, gv = attention_back_call(
        first, q, k, v, att, inv_tot, grad_branch_all, proj_own, seg_col, seg_row, cosine, sine
    )
    grad_qkv = jnp.concatenate([gq, gk, gv], axis=1)
    qkv_term = jnp.einsum("td,tm->dm", normed, grad_qkv, preferred_element_type=f32)
    grad_normed = jnp.einsum(
        "tm,dm->td", grad_qkv, qkv_full[:, :cols], preferred_element_type=f32
    )
    gain_one_term = jnp.sum(grad_normed * x_all.astype(f32) * inv_one, axis=0)
    grad_normed_own = group_reduce(lambda r: mine(grad_normed, r))
    inputs = tokens.astype(f32)
    inv_one_own = own(inv_one)
    scaled_one = grad_normed_own * gain_one
    grad_inputs = (
        grad_hidden
        + inv_one_own * scaled_one
        - inputs
        * (inv_one_own * inv_one_own * inv_one_own)
        * jnp.mean(scaled_one * inputs, axis=-1, keepdims=True)
    )
    token_grad = grad_inputs.astype(bf16)

    small = jnp.concatenate(
        [
            router_term[:, :experts_all],
            gain_one_term[:, None],
            gain_two_term[:, None],
            jnp.zeros((dim, PACK - experts_all - 2), f32),
        ],
        axis=1,
    )
    dense_term = jnp.concatenate([qkv_term, small], axis=1).reshape(n, groups, lines, wide)
    dense_term = jnp.concatenate(
        [dense_term[:, e] for e in range(groups)] + [proj_term.reshape(n, lines, dim)], axis=2
    ).astype(bf16)
    dense_term = dense_term.reshape(n, 2, lines // 2, groups * wide + dim)

    def pick_dense(offset, lo, hi):
        chunk = lax.dynamic_index_in_dim(dense_term, ring.device(offset), 0, keepdims=False)
        return chunk[lo:hi]

    dense_sum = ring.reduce(pick_dense).reshape(lines, groups * wide + dim)
    to = jnp.stack([dense_sum[:, e * wide : (e + 1) * wide] for e in range(groups)])
    give = lambda r: lax.dynamic_index_in_dim(to, member ^ r, 0, keepdims=False)
    got = [give(0)] + [xor_send(give(r), r) for r in range(1, groups)]
    small_sum = sum(g[:, cols:] for g in got)
    stacked = in_order([g[:, :cols] for g in got], member, 1)
    qkv_grad = jnp.concatenate(
        [stacked[:, j * cols : j * cols + qw] for j in range(groups)]
        + [stacked[:, j * cols + qw : j * cols + qw + kw] for j in range(groups)]
        + [stacked[:, j * cols + qw + kw : (j + 1) * cols] for j in range(groups)],
        axis=1,
    )
    router_grad = small_sum[:, :experts_all]
    gains_grad = small_sum[:, experts_all : experts_all + 2].T
    proj_grad = lax.ppermute(
        dense_sum[:, groups * wide :],
        ("dp", "expert"),
        [(d * groups + m, m * n + d) for d in range(n) for m in range(groups)],
    )

    gate_rows = gate_up_weight.shape[0]
    sums = []
    for s in range(0, experts_here, 2):
        pair = local_grads[s : s + 2]

        def pick(offset, lo, hi, pair=pair):
            at = ring.device(offset)
            return jnp.concatenate(
                [lax.dynamic_index_in_dim(p, at, 1, keepdims=False) for p in pair[lo:hi]]
            )

        sums.append(ring.reduce(pick))
    expert_sum = jnp.moveaxis(jnp.concatenate(sums), 0, 1)
    gate_up_grad, down_grad = expert_sum[:gate_rows], expert_sum[gate_rows:]

    qkv_new = adamw(qkv_weight, qkv_grad, qkv_mean, qkv_square, learn_rate, weight_decay)
    proj_new = adamw(proj_weight, proj_grad, proj_mean, proj_square, learn_rate, weight_decay)
    router_new = adamw(
        router_weight, router_grad, router_mean, router_square, learn_rate, weight_decay
    )
    gains_new = adamw(norm_gains, gains_grad, gains_mean, gains_square, gain_rate, 0.0)
    gate_up_new = adamw(
        gate_up_weight, gate_up_grad, gate_up_mean, gate_up_square, learn_rate, weight_decay
    )
    down_new = adamw(down_weight, down_grad, down_mean, down_square, learn_rate, weight_decay)
    return (
        layer_out,
        token_grad,
        qkv_grad,
        *qkv_new,
        proj_grad,
        *proj_new,
        router_grad,
        *router_new,
        gains_grad,
        *gains_new,
        gate_up_grad,
        *gate_up_new,
        down_grad,
        *down_new,
    )


def solution(mesh):
    rows = P(("dp", "expert"), None)
    gains = P(None, ("dp", "expert"))
    expert = P("dp", "expert", None)
    in_specs = (rows, rows, P("dp"), rows) + (rows,) * 9 + (gains,) * 3 + (expert,) * 6
    out_specs = (rows, rows) + (rows,) * 12 + (gains,) * 4 + (expert,) * 8
    return jax.shard_map(
        on_device, mesh=mesh, in_specs=in_specs, out_specs=out_specs, check_vma=False
    )
```
